128 devices in a mesh: mp: 8 (over x, y_hi), fsdp: 16 (over z, y_lo, core).
Axes of the slice: x: 4, y: 4 (y_hi: 2, y_lo: 2; y = y_hi * 2 + y_lo), z: 4, core: 2. Of those that a mesh axis runs over, the one named last changes fastest.
Arguments:
- weights: bfloat16 [8, 4096, 14336], P('mp', None, 'fsdp'), may hold values from -6 to 6
- acts: bfloat16 [8, 1024, 4096], P('mp', 'fsdp'), may hold values from -6 to 6
- cotangent: bfloat16 [8, 1024, 14336], P('mp', 'fsdp'), may hold values from -0.26367188 to 0.26367188
- token_ids: int32 [8, 1024], P('mp', 'fsdp'), may hold values from 0 to 31999, as said below
Outputs:
- merged: bfloat16 [4096, 14336], P('mp', 'fsdp')
The draws below stay inside these ranges and needn't reach their ends.
Inputs may be any that keep to these rules, and one draw needn't show every extreme that they name: `token_ids`: each calibration sequence of 512 tokens holds live ids of 1 to 31999 first and then padding ids 0, at most 256 of them.
All inputs are finite; a program needn't handle non-finite values.
Results may differ from the reference program's by a relative error of at most 0.001.
Values may be sent and summed in bfloat16 or wider, within the bound.
No kernel may reach another device: no remote copies, remote signals or barrier semaphores. Data moves between devices by JAX's collectives and lax.ppermute only.
A program may use at most 128 MiB of HBM per device.

```python
import jax
import jax.numpy as jnp
from jax import lax

DW = 4096
FFW = 14336
SEQ = 512
SEQS = 2
VOCAB = 32000
TOKENS = 1024
MODELS = 8


def draw_token_ids(key, part):
    first_key, second_key = jax.random.split(jax.random.fold_in(key, 17))
    lengths = jax.random.randint(first_key, (MODELS, SEQS, 1), SEQ // 2, SEQ + 1)
    positions = jnp.arange(SEQ, dtype=jnp.int32)[None, None, :]
    values = jax.random.randint(second_key, (MODELS, SEQS, SEQ), 1, VOCAB)
    return jnp.where(positions < lengths, values, 0).reshape(MODELS, TOKENS).astype(jnp.int32)


def level_of(rng, dims, cuts, low, high):
    factor_of, own = 1.0, jax.random.fold_in(rng, 6)
    for dim, blocks in cuts:
        steps = jnp.exp(jax.random.uniform(jax.random.fold_in(own, dim), (blocks,), jnp.float32, low / len(cuts), high / len(cuts)))
        factor_of = factor_of * jnp.repeat(steps, dims[dim] // blocks).reshape([-1 if axis == dim else 1 for axis in range(len(dims))])
    return factor_of


def centred(own_key, shape, width, reach, cuts=(), kind=jnp.bfloat16):
    loudness = level_of(own_key, shape, cuts, -0.22, 0.18) if cuts else 1.0
    result = jax.random.normal(own_key, shape, jnp.float32) * width * loudness
    return jnp.minimum(jnp.maximum(result, -reach), reach).astype(kind)


def setup_inputs(seed: int = 0) -> dict:
    key_of = jax.random.split(jax.random.key(seed), 5)
    weights = centred(key_of[0], (MODELS, DW, FFW), 1.0, 6.0, ((0, 8), (2, 16)))
    acts = centred(key_of[1], (MODELS, TOKENS, DW), 1.0, 6.0, ((0, 8), (1, 16)))
    cotangent = centred(key_of[2], (MODELS, TOKENS, FFW), (1.0 / SEQ ** 0.5), 0.26367188, ((0, 8), (1, 16)))
    token_ids = draw_token_ids(jax.random.fold_in(key_of[4], 71), 0)
    return {"weights": weights, "acts": acts, "cotangent": cotangent, "token_ids": token_ids}


damping = 0.1


def reference(weights, acts, cotangent, token_ids):
    def add_model(totals, inputs):
        numerator, denominator = totals
        model_weights, model_acts, model_grads, model_ids = inputs
        live_rows = (model_ids > 0).astype(jnp.bfloat16)
        masked = model_grads * live_rows[:, None]
        fisher = jnp.zeros((DW, FFW), jnp.float32)
        for sequence in range(SEQS):
            acts_part = model_acts[sequence * SEQ:(sequence + 1) * SEQ]
            grads_part = masked[sequence * SEQ:(sequence + 1) * SEQ]
            grads = jnp.dot(acts_part.T, grads_part, preferred_element_type=jnp.float32)
            fisher = fisher + grads * grads
        importance = fisher / SEQS + damping
        return (numerator + importance * model_weights.astype(jnp.float32), denominator + importance), None

    start = (jnp.zeros((DW, FFW), jnp.float32), jnp.zeros((DW, FFW), jnp.float32))
    (numerator, denominator), _ = lax.scan(add_model, start, (weights, acts, cotangent, token_ids))
    return (numerator / denominator).astype(jnp.bfloat16)
```

```python
import jax
import jax.numpy as jnp
from jax import lax
from jax.experimental import pallas as pl
from jax.experimental.pallas import tpu as pltpu
from jax.sharding import Mesh
from jax.sharding import PartitionSpec as P

SEQS = 2
damping = 0.1


X, YH, Z, YL, CORE = 4, 2, 4, 2, 2
FS = Z * YL * CORE
CHUNKS = ((0, 256), (256, 384), (640, 256))
RTILE = 128


def ring(axis, size, step):
    return lambda a: lax.ppermute(a, axis, [(i, (i + step) % size) for i in range(size)])


def transpose_kernel(a_ref, out_ref):
    fs, _, t, r = a_ref.shape
    out_ref[0] = a_ref[:, 0].reshape(fs * t, r).T


def transposed(a):
    fs, m, t, r = a.shape
    return pl.pallas_call(
        transpose_kernel,
        out_shape=jax.ShapeDtypeStruct((m, r, fs * t), a.dtype),
        grid=(m,),
        in_specs=[pl.BlockSpec((fs, 1, t, r), lambda i: (0, i, 0, 0))],
        out_specs=pl.BlockSpec((1, r, fs * t), lambda i: (i, 0, 0)),
        name="transpose_acts",
    )(a)


def sums(a_ref, c_refs, w_refs):
    seq = a_ref.shape[2] // SEQS
    numerator = denominator = None
    for m in range(X):
        fisher = None
        for s in range(SEQS):
            if m < X - 1:
                c = c_refs[m][s * seq:(s + 1) * seq, :]
            else:
                c = c_refs[m + s][...]
            g = jnp.dot(a_ref[m, :, s * seq:(s + 1) * seq], c, preferred_element_type=jnp.float32)
            fisher = g * g if fisher is None else fisher + g * g
        importance = fisher / SEQS + damping
        weighted = importance * w_refs[m][...].astype(jnp.float32)
        numerator = weighted if numerator is None else numerator + weighted
        denominator = importance if denominator is None else denominator + importance
    return numerator, denominator


def partial_kernel(a_ref, *refs):
    numerator, denominator = sums(a_ref, refs[:5], refs[5:9])
    out_ref = refs[9]
    out_ref[0] = numerator
    out_ref[1] = denominator


def merge_kernel(a_ref, *refs):
    numerator, denominator = sums(a_ref, refs[:5], refs[5:9])
    other_ref, out_ref = refs[9], refs[10]
    out_ref[...] = ((numerator + other_ref[0]) / (denominator + other_ref[1])).astype(out_ref.dtype)


def specs(a, cs, ws):
    tokens = a.shape[2]
    return (
        [pl.BlockSpec((X, RTILE, tokens), lambda i: (0, i, 0))]
        + [pl.BlockSpec(c.shape, lambda i: (0, 0)) for c in cs]
        + [pl.BlockSpec((RTILE, w.shape[1]), lambda i: (i, 0)) for w in ws]
    )


def partial_sums(a, cs, ws):
    rows, cols = ws[0].shape
    return pl.pallas_call(
        partial_kernel,
        out_shape=jax.ShapeDtypeStruct((2, rows, cols), jnp.float32),
        grid=(rows // RTILE,),
        in_specs=specs(a, cs, ws),
        out_specs=pl.BlockSpec((2, RTILE, cols), lambda i: (0, i, 0)),
        name="partial_sums",
    )(a, *cs, *ws)


def merge(a, cs, ws, other):
    rows, cols = ws[0].shape
    return pl.pallas_call(
        merge_kernel,
        out_shape=jax.ShapeDtypeStruct((rows, cols), jnp.bfloat16),
        grid=(rows // RTILE,),
        in_specs=specs(a, cs, ws) + [pl.BlockSpec((2, RTILE, cols), lambda i: (0, i, 0))],
        out_specs=pl.BlockSpec((RTILE, cols), lambda i: (i, 0)),
        name="merge",
    )(a, *cs, *ws, other)


def per_device(weights, acts, cotangent, token_ids):
    x = lax.axis_index("x")
    y = lax.axis_index("yh")
    rows = weights.shape[1] // (X * YH)
    cols = weights.shape[2]
    plus = ring("x", X, 1)
    minus = ring("x", X, -1)
    across = ring("x", X, 2)
    swap = ring("yh", YH, 1)

    live = (token_ids[0] > 0).astype(acts.dtype)[:, None]

    def at_x(step):
        return lax.rem(x + step, X) * YH

    def spread(piece):
        return [
            piece(at_x(0)),
            plus(piece(at_x(1))),
            minus(piece(at_x(3))),
            across(piece(at_x(2))),
        ]

    def acts_for(half):
        def piece(base):
            cut = lax.dynamic_slice_in_dim(acts[0], (base + half) * rows, rows, 1)
            return cut * live

        pieces = jnp.stack(spread(piece))
        return lax.all_gather(pieces, ("z", "yl", "c"), axis=0, tiled=False)

    def weights_for(half, start, width):
        def piece(base):
            return lax.dynamic_slice(weights[0], ((base + half) * rows, start), (rows, width))

        return spread(piece)

    a_other = acts_for(1 - y)
    a_own = acts_for(y)
    w_other = [weights_for(1 - y, *chunk) for chunk in CHUNKS]

    columns = lax.all_to_all(cotangent[0], ("z", "yl", "c"), split_axis=1, concat_axis=0, tiled=True)
    half_tokens = columns.shape[0] // 2
    grads = []
    for start, width in CHUNKS:
        own = columns[:, start:start + width]
        left = plus(own)
        right = minus(own)
        far0 = plus(left[:half_tokens])
        far1 = minus(right[half_tokens:])
        grads.append([own, left, right, far0, far1])

    w_own = [weights_for(y, *chunk) for chunk in CHUNKS]

    a_other = transposed(a_other)
    a_own = transposed(a_own)
    sent = [swap(partial_sums(a_other, g, w)) for g, w in zip(grads, w_other)]
    outs = [merge(a_own, g, w, s) for g, w, s in zip(grads, w_own, sent)]
    return jnp.concatenate(outs, axis=1)


def solution(mesh):
    fine = Mesh(mesh.devices.reshape(X, YH, Z, YL, CORE), ("x", "yh", "z", "yl", "c"))
    mp, fsdp = ("x", "yh"), ("z", "yl", "c")
    return jax.shard_map(
        per_device,
        mesh=fine,
        in_specs=(
            P(mp, None, fsdp),
            P(mp, fsdp, None),
            P(mp, fsdp, None),
            P(mp, fsdp),
        ),
        out_specs=P(mp, fsdp),
        check_vma=False,
    )
```

```python
import functools

import jax
import jax.numpy as jnp
from jax import lax
from jax.experimental import pallas as pl
from jax.sharding import Mesh
from jax.sharding import PartitionSpec as P

SEQS = 2
damping = 0.1


X, YH, Z, YL, CORE = 4, 2, 4, 2, 2
FS = Z * YL * CORE
CHUNKS = ((0, 384), (384, 256), (640, 256))
RTILE = 256


def transpose_kernel(a_ref, out_ref):
    fs, _, t, r = a_ref.shape
    out_ref[0] = a_ref[:, 0].reshape(fs * t, r).T


def transposed(a):
    fs, m, t, r = a.shape
    return pl.pallas_call(
        transpose_kernel,
        out_shape=jax.ShapeDtypeStruct((m, r, fs * t), a.dtype),
        grid=(m,),
        in_specs=[pl.BlockSpec((fs, 1, t, r), lambda i: (0, i, 0, 0))],
        out_specs=pl.BlockSpec((1, r, fs * t), lambda i: (i, 0, 0)),
        name="transpose_acts",
    )(a)


def sums(a_ref, c_refs, w_refs, at):
    seq = a_ref.shape[2] // SEQS
    width = c_refs[0].shape[1]
    numerator = denominator = None
    for m in range(X):
        fisher = None
        for s in range(SEQS):
            if m < X - 1:
                c = c_refs[m][s * seq:(s + 1) * seq, :]
            else:
                c = c_refs[m + s][...]
            g = jnp.dot(a_ref[m, :, s * seq:(s + 1) * seq], c, preferred_element_type=jnp.float32)
            fisher = g * g if fisher is None else fisher + g * g
        importance = fisher / SEQS + damping
        weighted = importance * w_refs[m][:, at:at + width].astype(jnp.float32)
        numerator = weighted if numerator is None else numerator + weighted
        denominator = importance if denominator is None else denominator + importance
    return numerator, denominator


def partial_kernel(at, a_ref, *refs):
    numerator, denominator = sums(a_ref, refs[:5], refs[5:9], at)
    out_ref = refs[9]
    out_ref[0] = numerator
    out_ref[1] = denominator


def merge_kernel(at, a_ref, *refs):
    numerator, denominator = sums(a_ref, refs[:5], refs[5:9], at)
    other_ref, earlier, out_ref = refs[9], refs[10:-1], refs[-1]
    merged = (numerator + other_ref[0]) / (denominator + other_ref[1])
    column = 0
    for ref in earlier:
        out_ref[:, column:column + ref.shape[1]] = ref[...]
        column += ref.shape[1]
    out_ref[:, column:column + merged.shape[1]] = merged.astype(out_ref.dtype)


def specs(a, cs, ws):
    tokens = a.shape[2]
    return (
        [pl.BlockSpec((X, RTILE, tokens), lambda i: (0, i, 0))]
        + [pl.BlockSpec(c.shape, lambda i: (0, 0)) for c in cs]
        + [pl.BlockSpec((RTILE, w.shape[1]), lambda i: (i, 0)) for w in ws]
    )


def partial_sums(a, cs, ws, at):
    rows, cols = ws[0].shape[0], cs[0].shape[1]
    return pl.pallas_call(
        functools.partial(partial_kernel, at),
        out_shape=jax.ShapeDtypeStruct((2, rows, cols), jnp.float32),
        grid=(rows // RTILE,),
        in_specs=specs(a, cs, ws),
        out_specs=pl.BlockSpec((2, RTILE, cols), lambda i: (0, i, 0)),
        name="partial_sums",
    )(a, *cs, *ws)


def merge(a, cs, ws, at, other, earlier):
    rows, cols = ws[0].shape[0], cs[0].shape[1]
    width = cols + sum(e.shape[1] for e in earlier)
    return pl.pallas_call(
        functools.partial(merge_kernel, at),
        out_shape=jax.ShapeDtypeStruct((rows, width), jnp.bfloat16),
        grid=(rows // RTILE,),
        in_specs=specs(a, cs, ws)
        + [pl.BlockSpec((2, RTILE, cols), lambda i: (0, i, 0))]
        + [pl.BlockSpec((RTILE, e.shape[1]), lambda i: (i, 0)) for e in earlier],
        out_specs=pl.BlockSpec((RTILE, width), lambda i: (i, 0)),
        name="merge",
    )(a, *cs, *ws, other, *earlier)


def send(axis, size, step, value):
    return lax.ppermute(value, axis, [(i, (i + step) % size) for i in range(size)])


def per_device(weights, acts, cotangent, token_ids):
    x = lax.axis_index("x")
    y = lax.axis_index("yh")
    rows = weights.shape[1] // (X * YH)
    cols = weights.shape[2]
    fsdp = ("z", "yl", "c")
    tokens = cotangent.shape[1]

    live = (token_ids[0] > 0).astype(acts.dtype)[:, None]

    def spread(half, piece):
        def at_x(step):
            return (lax.rem(x + step, X) * YH + half) * rows

        return [
            piece(at_x(0)),
            send("x", X, 1, piece(at_x(1))),
            send("x", X, -1, piece(at_x(3))),
            send("x", X, 2, piece(at_x(2))),
        ]

    def acts_piece(base):
        return lax.dynamic_slice_in_dim(acts[0], base, YH * rows, 1) * live

    def gathered(pieces, half):
        cut = lax.dynamic_slice_in_dim(pieces, half * rows, rows, 2)
        return lax.all_gather(cut, fsdp, axis=0, tiled=False)

    def weights_for(half, start, width):
        return spread(half, lambda base: lax.dynamic_slice(weights[0], (base, start), (rows, width)))

    def columns_for(start, width):
        cut = cotangent[0].reshape(tokens, FS, cols)[:, :, start:start + width]
        moved = lax.all_to_all(cut, fsdp, split_axis=1, concat_axis=0, tiled=True)
        return moved.reshape(FS * tokens, width)

    def near(own):
        return own, send("x", X, 1, own), send("x", X, -1, own)

    def far(own, left, right):
        half = own.shape[0] // 2
        far0 = send("x", X, 1, left[:half])
        far1 = send("x", X, -1, right[half:])
        return [own, left, right, far0, far1]

    def partial(n, grads):
        return partial_sums(a_other, grads, wp[n], 0)

    def after(value, arrays):
        return lax.optimization_barrier((value, arrays))[1]

    first, rest = CHUNKS[0], (CHUNKS[1][0], cols - CHUNKS[1][0])
    pieces = jnp.stack(spread(0, acts_piece))
    a_other = gathered(pieces, 1 - y)
    a_own = gathered(pieces, y)
    wp = [weights_for(1 - y, *chunk) for chunk in CHUNKS]
    c0 = columns_for(*first)
    c12 = columns_for(*rest)
    grads = [far(*near(c0))]
    nears = []
    for n, (start, width) in enumerate(CHUNKS[1:], 1):
        at = start - rest[0]
        nears.append(near(c12[:, at:at + width]))

    last = CHUNKS[-1]
    wo = [weights_for(y, 0, last[0]), weights_for(y, *last)]

    a_other = transposed(a_other)
    a_own = transposed(a_own)
    partials = [partial(0, grads[0])]
    for n in (1, 2):
        grads.append(far(*after(partials[0], nears[n - 1])))
    partials += [partial(n, grads[n]) for n in (1, 2)]
    sent = [send("yh", YH, 1, p) for p in partials]
    outs = []
    for n, (start, width) in enumerate(CHUNKS):
        final = n == len(CHUNKS) - 1
        w, at = (wo[1], 0) if final else (wo[0], start)
        outs.append(merge(a_own, grads[n], w, at, sent[n], outs if final else []))
    return outs[-1]


def solution(mesh):
    fine = Mesh(mesh.devices.reshape(X, YH, Z, YL, CORE), ("x", "yh", "z", "yl", "c"))
    mp, fsdp = ("x", "yh"), ("z", "yl", "c")

    return jax.shard_map(
        per_device,
        mesh=fine,
        in_specs=(
            P(mp, None, fsdp),
            P(mp, fsdp, None),
            P(mp, fsdp, None),
            P(mp, fsdp),
        ),
        out_specs=P(mp, fsdp),
        check_vma=False,
    )
```

```python
import functools

import jax
import jax.numpy as jnp
from jax import lax
from jax.experimental import pallas as pl
from jax.experimental.pallas import tpu as pltpu
from jax.sharding import Mesh
from jax.sharding import PartitionSpec as P

SEQS = 2
damping = 0.1


X, YH, Z, YL, CORE = 4, 2, 4, 2, 2
FS = Z * YL * CORE
CHUNKS = ((0, 384), (384, 256), (640, 256))
RTILE = 256


VMEM_LIMIT = 24 * 1024 * 1024


def transpose_kernel(at_ref, *refs):
    blocks, out_ref, rows_ref = refs[:-2], refs[-2], refs[-1]
    models, tokens = blocks[0].shape[:2]
    for m in range(models):
        for n in range(YL):
            yl = lax.rem(at_ref[1] + n, YL)
            for k, step in enumerate((0, 3, 1, 2)):
                z = lax.rem(at_ref[0] + step, Z)
                rows_ref[m, z * YL + yl] = blocks[n * Z + k][m]
        turned = rows_ref[m].reshape(rows_ref.shape[1] * tokens, rows_ref.shape[3])
        out_ref[m] = turned.T


def in_vmem(kernel, here, arrays, out_shape, scratch=()):
    return pl.pallas_call(
        kernel,
        out_shape=out_shape,
        in_specs=[pl.BlockSpec(memory_space=pltpu.SMEM)]
        + [pl.BlockSpec(memory_space=pltpu.VMEM) for _ in arrays],
        out_specs=pl.BlockSpec(memory_space=pltpu.VMEM),
        scratch_shapes=list(scratch),
        compiler_params=pltpu.CompilerParams(vmem_limit_bytes=VMEM_LIMIT),
    )(here, *arrays)


def transposed(here, blocks):
    m, t, r = blocks[0].shape
    dtype = blocks[0].dtype
    return in_vmem(
        transpose_kernel, here, blocks,
        jax.ShapeDtypeStruct((m, r, Z * YL * t), dtype),
        [pltpu.VMEM((m, Z * YL, t, r), dtype)],
    )


def sums(at_ref, a_refs, c_refs, w_refs, at, row, width):
    half = a_refs[0].shape[2] // SEQS
    tile = slice(row, row + RTILE)
    numerator = denominator = None
    for m in range(X):
        fisher = None
        for s in range(SEQS):
            g = None
            for n, a_ref in enumerate(a_refs):
                core = at_ref[2] if n == 0 else 1 - at_ref[2]
                c_ref, k = c_refs[m][s]
                c = c_ref[k, :, core].reshape(half, width)
                a = a_ref[m, tile, s * half:(s + 1) * half]
                part = jnp.dot(a, c, preferred_element_type=jnp.float32)
                g = part if g is None else g + part
            fisher = g * g if fisher is None else fisher + g * g
        importance = fisher / SEQS + damping
        weighted = importance * w_refs[m][tile, at:at + width].astype(jnp.float32)
        numerator = weighted if numerator is None else numerator + weighted
        denominator = importance if denominator is None else denominator + importance
    return numerator, denominator


def compute_kernel(layout, at, merging, at_ref, *refs):
    a_refs, refs = refs[:2], refs[2:]
    count = 1 + max(n for pair in layout for n, _ in pair)
    arrays, refs = refs[:count], refs[count:]
    w_refs, refs = refs[:X], refs[X:]
    c_refs = [[(arrays[n], k) for n, k in pair] for pair in layout]
    width = arrays[0].shape[-1]
    rows = w_refs[0].shape[0]
    out_ref = refs[-1]
    for row in range(0, rows, RTILE):
        tile = slice(row, row + RTILE)
        numerator, denominator = sums(at_ref, a_refs, c_refs, w_refs, at, row, width)
        if not merging:
            out_ref[0, tile] = numerator
            out_ref[1, tile] = denominator
            continue
        other_ref, earlier = refs[0], refs[1:-1]
        merged = (numerator + other_ref[0, tile]) / (denominator + other_ref[1, tile])
        column = 0
        for ref in earlier:
            out_ref[tile, column:column + ref.shape[1]] = ref[tile]
            column += ref.shape[1]
        out_ref[tile, column:column + width] = merged.astype(out_ref.dtype)


def partial_sums(here, a, grads, ws, at):
    layout, cs = grads
    rows, cols = ws[0].shape[0], cs[0].shape[-1]
    return in_vmem(
        functools.partial(compute_kernel, layout, at, False), here, [*a, *cs, *ws],
        jax.ShapeDtypeStruct((2, rows, cols), jnp.float32),
    )


def merge(here, a, grads, ws, at, other, earlier):
    layout, cs = grads
    rows, cols = ws[0].shape[0], cs[0].shape[-1]
    width = cols + sum(e.shape[1] for e in earlier)
    return in_vmem(
        functools.partial(compute_kernel, layout, at, True), here,
        [*a, *cs, *ws, other, *earlier],
        jax.ShapeDtypeStruct((rows, width), jnp.bfloat16),
    )


def send(axis, size, step, value):
    return lax.ppermute(value, axis, [(i, (i + step) % size) for i in range(size)])


def per_device(weights, acts, cotangent, token_ids):
    x = lax.axis_index("x")
    y = lax.axis_index("yh")
    rows = weights.shape[1] // (X * YH)
    cols = weights.shape[2]
    fsdp = ("z", "yl", "c")
    tokens = cotangent.shape[1]

    here = jnp.stack([lax.axis_index("z"), lax.axis_index("yl"), lax.axis_index("c")])
    live = (token_ids[0] > 0).astype(acts.dtype)[:, None]

    def spread(half, piece):
        def at_x(step):
            return (lax.rem(x + step, X) * YH + half) * rows

        return [
            piece(at_x(0)),
            send("x", X, 1, piece(at_x(1))),
            send("x", X, -1, piece(at_x(3))),
            send("x", X, 2, piece(at_x(2))),
        ]

    def acts_piece(base):
        return lax.dynamic_slice_in_dim(acts[0], base, YH * rows, 1) * live

    def gathered(pieces, half):
        cut = lax.dynamic_slice_in_dim(pieces, half * rows, rows, 2)
        blocks = []
        for block in (cut, send("yl", YL, 1, cut)):
            blocks += [
                block, send("z", Z, 1, block), send("z", Z, -1, block), send("z", Z, 2, block)
            ]
        own = transposed(here, blocks)
        return own, send("c", CORE, 1, own)

    def weights_for(half, start, width, source=weights[0]):
        def piece(base):
            return lax.dynamic_slice(source, (base, start), (rows, width))

        return spread(half, piece)

    def columns_for(start, width):
        cut = cotangent[0].reshape(tokens, FS, cols)[:, :, start:start + width]
        moved = lax.all_to_all(cut, fsdp, split_axis=1, concat_axis=0, tiled=True)
        return moved.reshape(SEQS, Z // SEQS * YL, CORE, tokens, width)

    def near(own):
        return own, send("x", X, 1, own), send("x", X, -1, own)

    def far(own, left, right):
        far0 = send("x", X, 1, left[:1])
        far1 = send("x", X, -1, right[1:])
        layout = [[(0, 0), (0, 1)], [(1, 0), (1, 1)], [(2, 0), (2, 1)], [(3, 0), (4, 0)]]
        return layout, [own, left, right, far0, far1]

    def split(own):
        own0, own1 = own[:1], own[1:]
        left0 = send("x", X, 1, own0)
        right1 = send("x", X, -1, own1)
        left1 = send("x", X, 1, own1)
        right0 = send("x", X, -1, own0)
        far0 = send("x", X, 1, left0)
        far1 = send("x", X, -1, right1)
        layout = [[(0, 0), (0, 1)], [(1, 0), (2, 0)], [(3, 0), (4, 0)], [(5, 0), (6, 0)]]
        return layout, [own, left0, left1, right0, right1, far0, far1]

    def partial(n, grads):
        return partial_sums(here, a_other, grads, wp[n], 0)

    def after(value, arrays):
        return lax.optimization_barrier((value, arrays))[1]

    first, rest = CHUNKS[0], (CHUNKS[1][0], cols - CHUNKS[1][0])
    pieces = jnp.stack(spread(0, acts_piece))
    a_other = gathered(pieces, 1 - y)
    a_own = gathered(pieces, y)
    wp = [weights_for(1 - y, *chunk) for chunk in CHUNKS]
    c0 = columns_for(*first)
    c12 = columns_for(*rest)
    grads = [split(c0)]
    nears = []
    for n, (start, width) in enumerate(CHUNKS[1:], 1):
        at = start - rest[0]
        nears.append(near(c12[..., at:at + width]))

    partials = [partial(0, grads[0])]
    nears = after(partials[0], nears)
    late = after(partials[0], weights[0])
    grads += [far(*nears[n - 1]) for n in (1, 2)]
    last = CHUNKS[-1]
    wo = [weights_for(y, 0, last[0], late), weights_for(y, *last, late)]
    partials += [partial(n, grads[n]) for n in (1, 2)]
    sent = [send("yh", YH, 1, p) for p in partials]
    outs = []
    for n, (start, width) in enumerate(CHUNKS):
        final = n == len(CHUNKS) - 1
        w, at = (wo[1], 0) if final else (wo[0], start)
        outs.append(merge(here, a_own, grads[n], w, at, sent[n], outs if final else []))
    return outs[-1]


def solution(mesh):
    fine = Mesh(mesh.devices.reshape(X, YH, Z, YL, CORE), ("x", "yh", "z", "yl", "c"))
    mp, fsdp = ("x", "yh"), ("z", "yl", "c")

    return jax.shard_map(
        per_device,
        mesh=fine,
        in_specs=(
            P(mp, None, fsdp),
            P(mp, fsdp, None),
            P(mp, fsdp, None),
            P(mp, fsdp),
        ),
        out_specs=P(mp, fsdp),
        check_vma=False,
    )
```

```python
import functools

import jax
import jax.numpy as jnp
from jax import lax
from jax.experimental import pallas as pl
from jax.experimental.pallas import tpu as pltpu
from jax.sharding import Mesh
from jax.sharding import PartitionSpec as P

SEQS = 2
damping = 0.1


X, YH, Z, YL, CORE = 4, 2, 4, 2, 2
FS = Z * YL * CORE
CHUNKS = ((0, 384), (384, 256), (640, 256))
RTILE = 256


VMEM_LIMIT = 24 * 1024 * 1024


def in_vmem(kernel, here, arrays, out_shape, scratch=()):
    return pl.pallas_call(
        kernel,
        out_shape=out_shape,
        in_specs=[pl.BlockSpec(memory_space=pltpu.SMEM)]
        + [pl.BlockSpec(memory_space=pltpu.VMEM) for _ in arrays],
        out_specs=pl.BlockSpec(memory_space=pltpu.VMEM),
        scratch_shapes=list(scratch),
        compiler_params=pltpu.CompilerParams(vmem_limit_bytes=VMEM_LIMIT),
    )(here, *arrays)


def in_hbm(arrays):
    return [pltpu.with_memory_space_constraint(a, pltpu.HBM) for a in arrays]


def transpose_kernel(at_ref, *refs):
    blocks, (out_ref, rows_ref, turned_ref, sems) = refs[:-4], refs[-4:]
    copies = []
    for n in range(YL):
        yl = lax.rem(at_ref[1] + n, YL)
        for k, step in enumerate((0, 3, 1, 2)):
            z = lax.rem(at_ref[0] + step, Z)
            b = n * Z + k
            copies.append(pltpu.make_async_copy(blocks[b], rows_ref.at[:, z * YL + yl], sems.at[b]))
            copies[-1].start()
    for copy in copies:
        copy.wait()
    models, count, tokens, width = rows_ref.shape
    outs = []
    for m in range(models):
        turned_ref[m] = rows_ref[m].reshape(count * tokens, width).T
        outs.append(pltpu.make_async_copy(turned_ref.at[m], out_ref.at[m], sems.at[m]))
        outs[-1].start()
    for out in outs:
        out.wait()


def transposed(here, blocks):
    m, t, r = blocks[0].shape
    dtype = blocks[0].dtype
    return pl.pallas_call(
        transpose_kernel,
        out_shape=jax.ShapeDtypeStruct((m, r, Z * YL * t), dtype),
        in_specs=[pl.BlockSpec(memory_space=pltpu.SMEM)]
        + [pl.BlockSpec(memory_space=pltpu.HBM) for _ in blocks],
        out_specs=pl.BlockSpec(memory_space=pltpu.HBM),
        scratch_shapes=[
            pltpu.VMEM((m, Z * YL, t, r), dtype),
            pltpu.VMEM((m, r, Z * YL * t), dtype),
            pltpu.SemaphoreType.DMA((len(blocks),)),
        ],
        compiler_params=pltpu.CompilerParams(vmem_limit_bytes=VMEM_LIMIT),
        name="transpose_acts",
    )(here, *in_hbm(blocks))


def sums(at_ref, a_refs, c_refs, w_refs, at, row, width):
    half = a_refs[0].shape[2] // SEQS
    tile = slice(row, row + RTILE)
    numerator = denominator = None
    for m in range(X):
        fisher = None
        for s in range(SEQS):
            g = None
            for n, a_ref in enumerate(a_refs):
                core = at_ref[2] if n == 0 else 1 - at_ref[2]
                c_ref, k = c_refs[m][s]
                c = c_ref[k, :, core].reshape(half, width)
                a = a_ref[m, tile, s * half:(s + 1) * half]
                part = jnp.dot(a, c, preferred_element_type=jnp.float32)
                g = part if g is None else g + part
            fisher = g * g if fisher is None else fisher + g * g
        importance = fisher / SEQS + damping
        weighted = importance * w_refs[m][tile, at:at + width].astype(jnp.float32)
        numerator = weighted if numerator is None else numerator + weighted
        denominator = importance if denominator is None else denominator + importance
    return numerator, denominator


def compute_kernel(layout, at, merging, at_ref, *refs):
    a_refs, refs = refs[:2], refs[2:]
    count = 1 + max(n for pair in layout for n, _ in pair)
    arrays, refs = refs[:count], refs[count:]
    w_refs, refs = refs[:X], refs[X:]
    c_refs = [[(arrays[n], k) for n, k in pair] for pair in layout]
    width = arrays[0].shape[-1]
    rows = w_refs[0].shape[0]
    out_ref = refs[-1]
    for row in range(0, rows, RTILE):
        tile = slice(row, row + RTILE)
        numerator, denominator = sums(at_ref, a_refs, c_refs, w_refs, at, row, width)
        if not merging:
            out_ref[0, tile] = numerator
            out_ref[1, tile] = denominator
            continue
        other_ref, earlier = refs[0], refs[1:-1]
        merged = (numerator + other_ref[0, tile]) / (denominator + other_ref[1, tile])
        column = 0
        for ref in earlier:
            out_ref[tile, column:column + ref.shape[1]] = ref[tile]
            column += ref.shape[1]
        out_ref[tile, column:column + width] = merged.astype(out_ref.dtype)


def partial_sums(here, a, grads, ws, at):
    layout, cs = grads
    rows, cols = ws[0].shape[0], cs[0].shape[-1]
    return in_vmem(
        functools.partial(compute_kernel, layout, at, False), here, [*a, *cs, *ws],
        jax.ShapeDtypeStruct((2, rows, cols), jnp.float32),
    )


def merge(here, a, grads, ws, at, other, earlier):
    layout, cs = grads
    rows, cols = ws[0].shape[0], cs[0].shape[-1]
    width = cols + sum(e.shape[1] for e in earlier)
    return in_vmem(
        functools.partial(compute_kernel, layout, at, True), here,
        [*a, *cs, *ws, other, *earlier],
        jax.ShapeDtypeStruct((rows, width), jnp.bfloat16),
    )


def send(axis, size, step, value):
    return lax.ppermute(value, axis, [(i, (i + step) % size) for i in range(size)])


def per_device(weights, acts, cotangent, token_ids):
    x = lax.axis_index("x")
    y = lax.axis_index("yh")
    rows = weights.shape[1] // (X * YH)
    cols = weights.shape[2]
    fsdp = ("z", "yl", "c")
    tokens = cotangent.shape[1]

    here = jnp.stack([lax.axis_index("z"), lax.axis_index("yl"), lax.axis_index("c")])
    live = (token_ids[0] > 0).astype(acts.dtype)[:, None]

    def spread(half, piece):
        def at_x(step):
            return (lax.rem(x + step, X) * YH + half) * rows

        return [
            piece(at_x(0)),
            send("x", X, 1, piece(at_x(1))),
            send("x", X, -1, piece(at_x(3))),
            send("x", X, 2, piece(at_x(2))),
        ]

    def acts_piece(base):
        return lax.dynamic_slice_in_dim(acts[0], base, YH * rows, 1) * live

    def gathered(pieces, half):
        cut = lax.dynamic_slice_in_dim(pieces, half * rows, rows, 2)
        blocks = []
        for block in (cut, send("yl", YL, 1, cut)):
            blocks += [
                block, send("z", Z, 1, block), send("z", Z, -1, block), send("z", Z, 2, block)
            ]
        own = transposed(here, blocks)
        return own, send("c", CORE, 1, own)

    def weights_for(half, start, width, source=weights[0]):
        def piece(base):
            return lax.dynamic_slice(source, (base, start), (rows, width))

        return spread(half, piece)

    def columns_for(start, width):
        cut = cotangent[0].reshape(tokens, FS, cols)[:, :, start:start + width]
        moved = lax.all_to_all(cut, fsdp, split_axis=1, concat_axis=0, tiled=True)
        return moved.reshape(SEQS, Z // SEQS * YL, CORE, tokens, width)

    def near(own):
        return own, send("x", X, 1, own), send("x", X, -1, own)

    def far(own, left, right):
        near0, near1 = left[:1], right[1:]
        far0 = send("x", X, 1, near0)
        far1 = send("x", X, -1, near1)
        layout = [[(0, 0), (0, 1)], [(1, 0), (1, 1)], [(2, 0), (2, 1)], [(3, 0), (4, 0)]]
        return layout, [own, left, right, far0, far1]

    def split(own):
        own0, own1 = own[:1], own[1:]
        left0 = send("x", X, 1, own0)
        right1 = send("x", X, -1, own1)
        left1 = send("x", X, 1, own1)
        right0 = send("x", X, -1, own0)
        far0 = send("x", X, 1, left0)
        far1 = send("x", X, -1, right1)
        layout = [[(0, 0), (0, 1)], [(1, 0), (2, 0)], [(3, 0), (4, 0)], [(5, 0), (6, 0)]]
        return layout, [own, left0, left1, right0, right1, far0, far1]

    def partial(n, grads):
        return partial_sums(here, a_other, grads, wp[n], 0)

    def after(value, arrays):
        return lax.optimization_barrier((value, arrays))[1]

    first, rest = CHUNKS[0], (CHUNKS[1][0], cols - CHUNKS[1][0])
    pieces = jnp.stack(spread(0, acts_piece))
    a_other = gathered(pieces, 1 - y)
    a_own = gathered(pieces, y)
    wp = [weights_for(1 - y, *chunk) for chunk in CHUNKS]
    c0 = columns_for(*first)
    c12 = columns_for(*rest)
    grads = [split(c0)]
    partials = [partial(0, grads[0])]
    c12 = after(partials[0], c12)
    late = after(partials[0], weights[0])
    for n, (start, width) in enumerate(CHUNKS[1:], 1):
        at = start - rest[0]
        part = c12[..., at:at + width]
        grads.append(split(part) if n == 1 else far(*near(part)))
    wo = [weights_for(y, *chunk, late) for chunk in CHUNKS]
    partials += [partial(n, grads[n]) for n in (1, 2)]
    sent = [send("yh", YH, 1, p) for p in partials]
    outs = []
    for n, (start, width) in enumerate(CHUNKS):
        earlier = outs if n == len(CHUNKS) - 1 else []
        outs.append(merge(here, a_own, grads[n], wo[n], 0, sent[n], earlier))
    return outs[-1]


def solution(mesh):
    fine = Mesh(mesh.devices.reshape(X, YH, Z, YL, CORE), ("x", "yh", "z", "yl", "c"))
    mp, fsdp = ("x", "yh"), ("z", "yl", "c")

    return jax.shard_map(
        per_device,
        mesh=fine,
        in_specs=(
            P(mp, None, fsdp),
            P(mp, fsdp, None),
            P(mp, fsdp, None),
            P(mp, fsdp),
        ),
        out_specs=P(mp, fsdp),
        check_vma=False,
    )
```

```python
import functools

import jax
import jax.numpy as jnp
from jax import lax
from jax.experimental import pallas as pl
from jax.experimental.pallas import tpu as pltpu
from jax.sharding import Mesh
from jax.sharding import PartitionSpec as P

SEQS = 2
damping = 0.1


X, YH, Z, YL, CORE = 4, 2, 4, 2, 2
FS = Z * YL * CORE
CHUNKS = ((0, 384), (384, 256), (640, 256))
RTILE = 256


VMEM_LIMIT = 24 * 1024 * 1024


def in_vmem(kernel, here, arrays, out_shape, scratch=()):
    return pl.pallas_call(
        kernel,
        out_shape=out_shape,
        in_specs=[pl.BlockSpec(memory_space=pltpu.SMEM)]
        + [pl.BlockSpec(memory_space=pltpu.VMEM) for _ in arrays],
        out_specs=pl.BlockSpec(memory_space=pltpu.VMEM),
        scratch_shapes=list(scratch),
        compiler_params=pltpu.CompilerParams(vmem_limit_bytes=VMEM_LIMIT),
    )(here, *arrays)


def in_hbm(arrays):
    return [pltpu.with_memory_space_constraint(a, pltpu.HBM) for a in arrays]


def transpose_kernel(at_ref, *refs):
    blocks, (out_ref, rows_ref, turned_ref, sems) = refs[:-4], refs[-4:]
    copies = []
    for n in range(YL):
        yl = lax.rem(at_ref[1] + n, YL)
        for k, step in enumerate((0, 3, 1, 2)):
            z = lax.rem(at_ref[0] + step, Z)
            b = n * Z + k
            copies.append(pltpu.make_async_copy(blocks[b], rows_ref.at[:, z * YL + yl], sems.at[b]))
            copies[-1].start()
    for copy in copies:
        copy.wait()
    models, count, tokens, width = rows_ref.shape
    outs = []
    for m in range(models):
        turned_ref[m] = rows_ref[m].reshape(count * tokens, width).T
        outs.append(pltpu.make_async_copy(turned_ref.at[m], out_ref.at[m], sems.at[m]))
        outs[-1].start()
    for out in outs:
        out.wait()


def transposed(here, blocks):
    m, t, r = blocks[0].shape
    dtype = blocks[0].dtype
    return pl.pallas_call(
        transpose_kernel,
        out_shape=jax.ShapeDtypeStruct((m, r, Z * YL * t), dtype),
        in_specs=[pl.BlockSpec(memory_space=pltpu.SMEM)]
        + [pl.BlockSpec(memory_space=pltpu.HBM) for _ in blocks],
        out_specs=pl.BlockSpec(memory_space=pltpu.HBM),
        scratch_shapes=[
            pltpu.VMEM((m, Z * YL, t, r), dtype),
            pltpu.VMEM((m, r, Z * YL * t), dtype),
            pltpu.SemaphoreType.DMA((len(blocks),)),
        ],
        compiler_params=pltpu.CompilerParams(vmem_limit_bytes=VMEM_LIMIT),
        name="transpose_acts",
    )(here, *in_hbm(blocks))


def sums(at_ref, a_refs, c_refs, w_refs, at, row, width):
    half = a_refs[0].shape[2] // SEQS
    tile = slice(row, row + RTILE)
    numerator = denominator = None
    for m in range(X):
        fisher = None
        for s in range(SEQS):
            g = None
            for n, a_ref in enumerate(a_refs):
                core = at_ref[2] if n == 0 else 1 - at_ref[2]
                c_ref, k = c_refs[m][s]
                c = c_ref[k, :, core].reshape(half, width)
                a = a_ref[m, tile, s * half:(s + 1) * half]
                part = jnp.dot(a, c, preferred_element_type=jnp.float32)
                g = part if g is None else g + part
            fisher = g * g if fisher is None else fisher + g * g
        importance = fisher / SEQS + damping
        weighted = importance * w_refs[m][tile, at:at + width].astype(jnp.float32)
        numerator = weighted if numerator is None else numerator + weighted
        denominator = importance if denominator is None else denominator + importance
    return numerator, denominator


def compute_kernel(layout, at, merging, at_ref, *refs, done=None):
    a_refs, refs = refs[:2], refs[2:]
    count = 1 + max(n for pair in layout for n, _ in pair)
    arrays, refs = refs[:count], refs[count:]
    w_refs, refs = refs[:X], refs[X:]
    c_refs = [[(arrays[n], k) for n, k in pair] for pair in layout]
    width = arrays[0].shape[-1]
    rows = w_refs[0].shape[0]
    out_ref = refs[-1]
    for row in range(0, rows, RTILE):
        tile = slice(row, row + RTILE)
        numerator, denominator = sums(at_ref, a_refs, c_refs, w_refs, at, row, width)
        if not merging:
            out_ref[0, tile] = numerator
            out_ref[1, tile] = denominator
            continue
        other_ref = refs[0]
        merged = (numerator + other_ref[0, tile]) / (denominator + other_ref[1, tile])
        out_ref[tile] = merged.astype(out_ref.dtype)
        if done is not None:
            done(tile)


def last_kernel(layout, at, at_ref, *refs):
    refs, (out_ref, merged_ref, sems) = refs[:-3], refs[-3:]
    refs, earlier = refs[:-2], refs[-2:]
    copies, column = [], 0
    for n, ref in enumerate(earlier):
        part = out_ref.at[:, column:column + ref.shape[1]]
        copies.append(pltpu.make_async_copy(ref, part, sems.at[n]))
        copies[-1].start()
        column += ref.shape[1]

    def done(tile):
        part = out_ref.at[tile, column:column + merged_ref.shape[1]]
        copies.append(pltpu.make_async_copy(merged_ref.at[tile], part, sems.at[len(copies)]))
        copies[-1].start()

    compute_kernel(layout, at, True, at_ref, *refs, merged_ref, done=done)
    for copy in copies:
        copy.wait()


def partial_sums(here, a, grads, ws, at):
    layout, cs = grads
    rows, cols = ws[0].shape[0], cs[0].shape[-1]
    return in_vmem(
        functools.partial(compute_kernel, layout, at, False), here, [*a, *cs, *ws],
        jax.ShapeDtypeStruct((2, rows, cols), jnp.float32),
    )


def merge(here, a, grads, ws, at, other, earlier):
    layout, cs = grads
    rows, cols = ws[0].shape[0], cs[0].shape[-1]
    arrays = [*a, *cs, *ws, other, *earlier]
    width = cols + sum(e.shape[1] for e in earlier)
    out = jax.ShapeDtypeStruct((rows, width), jnp.bfloat16)
    if not earlier:
        return in_vmem(functools.partial(compute_kernel, layout, at, True), here, arrays, out)
    return pl.pallas_call(
        functools.partial(last_kernel, layout, at),
        out_shape=out,
        in_specs=[pl.BlockSpec(memory_space=pltpu.SMEM)]
        + [pl.BlockSpec(memory_space=pltpu.VMEM) for _ in arrays],
        out_specs=pl.BlockSpec(memory_space=pltpu.HBM),
        scratch_shapes=[
            pltpu.VMEM((rows, cols), out.dtype),
            pltpu.SemaphoreType.DMA((len(earlier) + rows // RTILE,)),
        ],
        compiler_params=pltpu.CompilerParams(vmem_limit_bytes=VMEM_LIMIT),
        name="merge",
    )(here, *arrays)


def send(axis, size, step, value):
    return lax.ppermute(value, axis, [(i, (i + step) % size) for i in range(size)])


def per_device(weights, acts, cotangent, token_ids):
    x = lax.axis_index("x")
    y = lax.axis_index("yh")
    rows = weights.shape[1] // (X * YH)
    cols = weights.shape[2]
    fsdp = ("z", "yl", "c")
    tokens = cotangent.shape[1]

    here = jnp.stack([lax.axis_index("z"), lax.axis_index("yl"), lax.axis_index("c")])
    live = (token_ids[0] > 0).astype(acts.dtype)[:, None]

    def spread(half, piece):
        def at_x(step):
            return (lax.rem(x + step, X) * YH + half) * rows

        return [
            piece(at_x(0)),
            send("x", X, 1, piece(at_x(1))),
            send("x", X, -1, piece(at_x(3))),
            send("x", X, 2, piece(at_x(2))),
        ]

    def acts_piece(base):
        return lax.dynamic_slice_in_dim(acts[0], base, YH * rows, 1) * live

    def gathered(pieces, half):
        cut = lax.dynamic_slice_in_dim(pieces, half * rows, rows, 2)
        blocks = []
        for block in (cut, send("yl", YL, 1, cut)):
            blocks += [
                block, send("z", Z, 1, block), send("z", Z, -1, block), send("z", Z, 2, block)
            ]
        own = transposed(here, blocks)
        return own, send("c", CORE, 1, own)

    def weights_for(half, start, width, source=weights[0]):
        def piece(base):
            return lax.dynamic_slice(source, (base, start), (rows, width))

        return spread(half, piece)

    def columns_for(start, width):
        cut = cotangent[0].reshape(tokens, FS, cols)[:, :, start:start + width]
        moved = lax.all_to_all(cut, fsdp, split_axis=1, concat_axis=0, tiled=True)
        return moved.reshape(SEQS, Z // SEQS * YL, CORE, tokens, width)

    def near(own):
        return own, send("x", X, 1, own), send("x", X, -1, own)

    def far(own, left, right):
        near0, near1 = left[:1], right[1:]
        far0 = send("x", X, 1, near0)
        far1 = send("x", X, -1, near1)
        layout = [[(0, 0), (0, 1)], [(1, 0), (1, 1)], [(2, 0), (2, 1)], [(3, 0), (4, 0)]]
        return layout, [own, left, right, far0, far1]

    def split(own):
        own0, own1 = own[:1], own[1:]
        left0 = send("x", X, 1, own0)
        right1 = send("x", X, -1, own1)
        left1 = send("x", X, 1, own1)
        right0 = send("x", X, -1, own0)
        far0 = send("x", X, 1, left0)
        far1 = send("x", X, -1, right1)
        layout = [[(0, 0), (0, 1)], [(1, 0), (2, 0)], [(3, 0), (4, 0)], [(5, 0), (6, 0)]]
        return layout, [own, left0, left1, right0, right1, far0, far1]

    def partial(n, grads):
        return partial_sums(here, a_other, grads, wp[n], 0)

    def after(value, arrays):
        return lax.optimization_barrier((value, arrays))[1]

    first, rest = CHUNKS[0], (CHUNKS[1][0], cols - CHUNKS[1][0])
    pieces = jnp.stack(spread(0, acts_piece))
    a_other = gathered(pieces, 1 - y)
    a_own = gathered(pieces, y)
    wp = [weights_for(1 - y, *chunk) for chunk in CHUNKS]
    c0 = columns_for(*first)
    c12 = columns_for(*rest)
    grads = [split(c0)]
    partials = [partial(0, grads[0])]
    c12 = after(partials[0], c12)
    late = after(partials[0], weights[0])
    for n, (start, width) in enumerate(CHUNKS[1:], 1):
        at = start - rest[0]
        part = c12[..., at:at + width]
        grads.append(split(part) if n == 1 else far(*near(part)))
    wo = [weights_for(y, *chunk, late) for chunk in CHUNKS]
    partials += [partial(n, grads[n]) for n in (1, 2)]
    sent = [send("yh", YH, 1, p) for p in partials]
    outs = []
    for n, (start, width) in enumerate(CHUNKS):
        earlier = outs if n == len(CHUNKS) - 1 else []
        outs.append(merge(here, a_own, grads[n], wo[n], 0, sent[n], earlier))
    return outs[-1]


def solution(mesh):
    fine = Mesh(mesh.devices.reshape(X, YH, Z, YL, CORE), ("x", "yh", "z", "yl", "c"))
    mp, fsdp = ("x", "yh"), ("z", "yl", "c")

    return jax.shard_map(
        per_device,
        mesh=fine,
        in_specs=(
            P(mp, None, fsdp),
            P(mp, fsdp, None),
            P(mp, fsdp, None),
            P(mp, fsdp),
        ),
        out_specs=P(mp, fsdp),
        check_vma=False,
    )
```
